512 devices in a mesh: mol: 128 (over z, y, core), traj: 4 (over x).
Axes of the slice: x: 4, y: 4, z: 16, core: 2. Of those that a mesh axis runs over, the one named last changes fastest.
Arguments:
- positions: float32 [64, 16384], P('traj', 'mol'), parts along dimension 0, may hold values from -1.2 to 1.2
- velocities: float32 [64, 16384], P('traj', 'mol'), parts along dimension 0, may hold values from -3 to 3
- amplitudes: float32 [4096, 64], P('mol', 'traj'), parts along dimension 1, may hold values from -6 to 6
- momenta: float32 [4096, 64], P('mol', 'traj'), parts along dimension 1, may hold values from -6 to 6
- sites: int32 [16384], P('mol'), may hold values from 0 to 32767
- wavevectors: int32 [4096], replicated, may hold values from 1 to 32767
- mode_freq: float32 [4096], P('mol'), may hold values from 0.5 to 2
- coupling: float32 [4096], P('mol'), may hold values from 0.0078125 to 0.03125
- depth: float32 [16384], P('mol'), may hold values from 0.5 to 2
- stiffness: float32 [16384], P('mol'), may hold values from 0.8 to 1.5
- dipole_slope: float32 [16384], P('mol'), may hold values from -4 to 4
Outputs:
- final_positions: float32 [64, 16384], P('traj', 'mol'), parts along dimension 0
- final_velocities: float32 [64, 16384], P('traj', 'mol'), parts along dimension 0
- final_amplitudes: float32 [4096, 64], P('mol', 'traj'), parts along dimension 1
- final_momenta: float32 [4096, 64], P('mol', 'traj'), parts along dimension 1
The draws below stay inside these ranges and needn't reach their ends.
There are 4 independent parts, one for each index of `traj`. The reference program is written for one: setup_inputs(seed, part) draws one part's arguments, and reference() takes and returns one part's arrays. A program takes and returns all parts, laid end to end along the dimension named above; an argument that names none is the same for every part. Nothing has to cross between parts.
All inputs are finite; a program needn't handle non-finite values.
Results may differ from the reference program's by a relative error of at most 0.0003.
Values sent between devices are 32-bit elements; how exact they have to be, the bound alone decides.
No kernel may reach another device: no remote copies, remote signals or barrier semaphores. Data moves between devices by JAX's collectives and lax.ppermute only.
A program may use at most 64 MiB of HBM per device.

```python
import math
import jax
import jax.numpy as jnp
from jax import lax

M = 4096
TR = 16
STEPS = 2
MOLECULES = 16384
LATTICE = 32768


def plant(array, stream_key, least, top_value):
    dims = array.shape
    spot = [jax.random.randint(jax.random.fold_in(stream_key, axis), (), 0, dims[axis]) for axis in range(len(dims))]
    array = array.at[tuple(spot)].set(least)
    longest = dims.index(max(dims))
    spot[longest] = (spot[longest] + 1) % dims[longest]
    return array.at[tuple(spot)].set(top_value)


def steps_of(rng, shape, pieces, smallest, top_value):
    level, own = 1.0, jax.random.fold_in(rng, 6)
    for dim, shards_of in pieces:
        draws = jnp.exp(jax.random.uniform(jax.random.fold_in(own, dim), (shards_of,), jnp.float32, smallest / len(pieces), top_value / len(pieces)))
        level = level * jnp.repeat(draws, shape[dim] // shards_of).reshape([-1 if axis == dim else 1 for axis in range(len(shape))])
    return level


def scatter_about(own_key, extent, deviation, limit, pieces=(), held_as=jnp.bfloat16):
    level = steps_of(own_key, extent, pieces, -0.22, 0.18) if pieces else 1.0
    array = jax.random.normal(own_key, extent, jnp.float32) * deviation * level
    return jnp.minimum(jnp.maximum(array, -limit), limit).astype(held_as)


def setup_inputs(seed: int = 0, part: int = 0) -> dict:
    keys = jax.random.split(jax.random.key(seed), 12)
    own_keys = jax.random.split(jax.random.fold_in(keys[11], part), 12)
    return {
        "positions": scatter_about(own_keys[0], (TR, MOLECULES), 0.3, 1.2, ((1, 128),), jnp.float32),
        "velocities": scatter_about(own_keys[1], (TR, MOLECULES), 0.5, 3.0, ((1, 128),), jnp.float32),
        "amplitudes": scatter_about(own_keys[2], (M, TR), 1.0, 6.0, ((0, 128),), jnp.float32),
        "momenta": scatter_about(own_keys[3], (M, TR), 1.0, 6.0, ((0, 128),), jnp.float32),
        "sites": plant(jax.random.randint(keys[4], (MOLECULES,), 0, LATTICE), jax.random.fold_in(keys[4], 1), 0, LATTICE - 1).astype(jnp.int32),
        "wavevectors": plant(jax.random.randint(keys[5], (M,), 1, LATTICE), jax.random.fold_in(keys[5], 1), 1, LATTICE - 1).astype(jnp.int32),
        "mode_freq": jnp.clip(jnp.exp(math.log(2.0) - 1.3862944 * jax.random.uniform(keys[6], (M,), jnp.float32) ** steps_of(keys[6], (M,), ((0, 128),), -0.2, 0.2)), 0.5, 2.0),
        "coupling": jnp.clip(jnp.exp(math.log(0.03125) - 1.3862944 * jax.random.uniform(keys[7], (M,), jnp.float32) ** steps_of(keys[7], (M,), ((0, 128),), -0.2, 0.2)), 0.0078125, 0.03125),
        "depth": jnp.clip(jnp.exp(math.log(2.0) - 1.3862944 * jax.random.uniform(keys[8], (MOLECULES,), jnp.float32) ** steps_of(keys[8], (MOLECULES,), ((0, 128),), -0.2, 0.2)), 0.5, 2.0),
        "stiffness": jnp.clip(0.8 + 0.7 * jax.random.uniform(keys[9], (MOLECULES,), jnp.float32) ** steps_of(keys[9], (MOLECULES,), ((0, 128),), -0.2, 0.2), 0.8, 1.5),
        "dipole_slope": scatter_about(keys[10], (MOLECULES,), 1.0, 4.0, ((0, 128),), jnp.float32),
    }


def phase_tile(waves, sites, lattice):
    high = sites // 256
    low = sites % 256
    first = (waves[:, None] * high[None, :]) % lattice
    residue = (first * 256 + waves[:, None] * low[None, :]) % lattice
    angle = residue.astype(jnp.float32) * (2.0 * math.pi / lattice)
    return jnp.sin(angle)


def reference(positions, velocities, amplitudes, momenta, sites, wavevectors, mode_freq, coupling, depth, stiffness, dipole_slope):
    step_time = 0.2
    block = 128
    wave_blocks = wavevectors.reshape(M // block, block)
    for step in range(STEPS):
        dipole = dipole_slope[None, :] * positions

        def drive_block(waves):
            tile = phase_tile(waves, sites, LATTICE)
            return lax.dot_general(tile, dipole, (((1,), (1,)), ((), ())), precision=lax.Precision.HIGHEST, preferred_element_type=jnp.float32)

        drive = lax.map(drive_block, wave_blocks).reshape(M, -1)
        momenta = momenta + step_time * (-(mode_freq * mode_freq)[:, None] * amplitudes - coupling[:, None] * drive)
        amplitudes = amplitudes + step_time * momenta
        weighted = (coupling[:, None] * amplitudes).reshape(M // block, block, -1)

        def add_pull(total, items):
            waves, piece = items
            tile = phase_tile(waves, sites, LATTICE)
            return total + lax.dot_general(piece, tile, (((0,), (0,)), ((), ())), precision=lax.Precision.HIGHEST, preferred_element_type=jnp.float32), None

        pull, unused = lax.scan(add_pull, jnp.zeros(positions.shape, jnp.float32), (wave_blocks, weighted))
        damped = jnp.exp(-stiffness[None, :] * positions)
        force = -2.0 * depth[None, :] * stiffness[None, :] * (1.0 - damped) * damped - dipole_slope[None, :] * pull
        velocities = velocities + step_time * force
        positions = positions + step_time * velocities
    return positions, velocities, amplitudes, momenta
```

```python
import functools

import jax
import jax.numpy as jnp
from jax import lax
from jax.experimental import pallas as pl
from jax.experimental.pallas import tpu as pltpu
from jax.sharding import PartitionSpec as P

STEP_TIME = 0.2
SINE = (25.132741928100586, -64.83582305908203, 67.0767593383789, -38.49842071533203, 14.06550407409668, -3.1933720111846924)
LANES = 128
F32, BF16 = jnp.float32, jnp.bfloat16


def split(x):
    high = x.astype(BF16)
    return high, (x - high.astype(F32)).astype(BF16)


def dot(a, b):
    return lax.dot_general(a, b, (((1,), (0,)), ((), ())), preferred_element_type=F32)


def sine_of(product, shift):
    turn = (product << shift).astype(F32) * (2.0**-32)
    square = turn * turn
    value = jnp.full_like(square, SINE[-1])
    for factor in SINE[-2::-1]:
        value = value * square + factor
    return turn * (0.25 - square) * value


def lane_groups(shape, width):
    return lax.broadcasted_iota(jnp.int32, shape, len(shape) - 1) // width


def block_diagonal(dipole, out_ref):
    traj, mols = dipole.shape
    pack = LANES // traj
    across = jnp.concatenate([dipole] * pack, axis=0).T
    high, low = split(across)
    high, low = high.astype(F32), low.astype(F32)
    group = lane_groups((mols, LANES), traj)
    for place in range(pack):
        rows = pl.ds(place * mols, mols)
        out_ref[rows, :LANES] = jnp.where(group == place, high, 0.0).astype(BF16)
        out_ref[rows, LANES:] = jnp.where(group == place, low, 0.0).astype(BF16)


def drive_rows(high_ref, low_ref, spread_ref):
    both = dot(high_ref[...], spread_ref[...])
    return both[:, :LANES] + both[:, LANES:] + dot(low_ref[...], spread_ref[:, :LANES])


def pull_of(rows_ref, high_ref, low_ref, traj, mols):
    high, low = split(rows_ref[...].T)
    pack = LANES // traj
    total = None
    for pair in range(pack // 2):
        rows = slice(pair * 2 * traj, (pair + 1) * 2 * traj)
        columns = pl.ds(pair * 2 * mols, 2 * mols)
        left = jnp.concatenate([high[rows], low[rows]], axis=0)
        first = dot(left, high_ref[:, columns])
        second = dot(high[rows], low_ref[:, columns])
        for side in range(2):
            cols = slice(side * mols, (side + 1) * mols)
            at = side * traj
            part = first[at : at + traj, cols] + first[2 * traj + at : 2 * traj + at + traj, cols] + second[at : at + traj, cols]
            total = part if total is None else total + part
    return total


def advance_bonds(positions, velocities, pull, depth, stiffness, dipole_slope):
    damped = jnp.exp(-stiffness * positions)
    force = -2.0 * depth * stiffness * (1.0 - damped) * damped - dipole_slope * pull
    velocities = velocities + STEP_TIME * force
    return positions + STEP_TIME * velocities, velocities


def first_kernel(shift, positions, slope, sites, waves, high_ref, low_ref, partial_ref, spread_ref):
    block_diagonal(slope[...] * positions[...], spread_ref)
    mols = sites.shape[1]
    pack = waves.shape[1]
    total = None
    for pair in range(pack // 2):
        for place in (2 * pair, 2 * pair + 1):
            columns = pl.ds(place * mols, mols)
            high, low = split(sine_of(waves[:, place : place + 1] * sites[...], shift))
            high_ref[:, columns] = high
            low_ref[:, columns] = low
        columns = pl.ds(2 * pair * mols, 2 * mols)
        both = dot(high_ref[:, columns], spread_ref[columns, :])
        part = both[:, :LANES] + both[:, LANES:] + dot(low_ref[:, columns], spread_ref[columns, :LANES])
        total = part if total is None else total + part
    partial_ref[...] = total


def pack_rows(block, traj):
    rows = block.shape[0]
    pack = LANES // traj
    wide = jnp.concatenate([block] * pack, axis=1)
    place = lax.broadcasted_iota(jnp.int32, wide.shape, 0) % pack
    wide = jnp.where(lane_groups(wide.shape, traj) == place, wide, 0.0)
    return wide.reshape(rows // pack, pack, LANES).sum(axis=1)


def unpack_rows(packed, traj):
    rows = packed.shape[0]
    pack = LANES // traj
    wide = jnp.broadcast_to(packed[:, None, :], (rows, pack, LANES)).reshape(rows * pack, LANES)
    place = lax.broadcasted_iota(jnp.int32, wide.shape, 0) % pack
    wide = jnp.where(lane_groups(wide.shape, traj) == place, wide, 0.0)
    total = wide[:, :traj]
    for group in range(1, pack):
        total = total + wide[:, group * traj : (group + 1) * traj]
    return total


def column_of(row, traj):
    modes = row.shape[1]
    spread = jnp.broadcast_to(row, (modes, modes))
    own = lax.broadcasted_iota(jnp.int32, (modes, modes), 0) == lax.broadcasted_iota(jnp.int32, (modes, modes), 1)
    return jnp.broadcast_to(jnp.where(own, spread, 0.0).sum(axis=1, keepdims=True), (modes, traj))


def modes_kernel(received, amplitudes, momenta, freq, coupling, amplitudes_out, momenta_out, weighted_ref):
    traj = amplitudes.shape[1]
    rows = amplitudes.shape[0] * traj // LANES
    pair = received[...].reshape(-1, 2 * rows, LANES).sum(axis=0)
    drive = unpack_rows(pair[:rows] + pair[rows:], traj)
    freq_of = column_of(freq[...], traj)
    coupling_of = column_of(coupling[...], traj)
    new_momenta = momenta[...] + STEP_TIME * (-(freq_of * freq_of) * amplitudes[...] - coupling_of * drive)
    new_amplitudes = amplitudes[...] + STEP_TIME * new_momenta
    momenta_out[...] = new_momenta
    amplitudes_out[...] = new_amplitudes
    weighted = pack_rows(coupling_of * new_amplitudes, traj)
    twice = jnp.concatenate([weighted, weighted], axis=0)
    copies = weighted_ref.shape[0] // (2 * rows)
    weighted_ref[...] = jnp.broadcast_to(twice[None], (copies, 2 * rows, LANES)).reshape(weighted_ref.shape)


def middle_kernel(rows, high_ref, low_ref, positions, velocities, depth, stiffness, slope, positions_out, velocities_out, partial_ref, spread_ref):
    pull = pull_of(rows, high_ref, low_ref, *positions.shape)
    new_positions, new_velocities = advance_bonds(
        positions[...], velocities[...], pull, depth[...], stiffness[...], slope[...]
    )
    positions_out[...] = new_positions
    velocities_out[...] = new_velocities
    block_diagonal(slope[...] * new_positions, spread_ref)
    partial_ref[...] = drive_rows(high_ref, low_ref, spread_ref)


def last_kernel(rows, high_ref, low_ref, positions, velocities, depth, stiffness, slope, positions_out, velocities_out):
    pull = pull_of(rows, high_ref, low_ref, *positions.shape)
    new_positions, new_velocities = advance_bonds(
        positions[...], velocities[...], pull, depth[...], stiffness[...], slope[...]
    )
    positions_out[...] = new_positions
    velocities_out[...] = new_velocities


def call(kernel, outs, name, scratch=(), interpret=False):
    return pl.pallas_call(
        kernel,
        out_shape=[jax.ShapeDtypeStruct(shape, dtype) for shape, dtype in outs],
        scratch_shapes=list(scratch),
        name=name,
        interpret=interpret,
        compiler_params=None if interpret else pltpu.CompilerParams(vmem_limit_bytes=48 << 20),
    )


def stages(traj, mols, modes, owned, shift, interpret=False):
    pack = LANES // traj
    rows = modes // pack
    phase = ((rows, pack * mols), BF16)
    packed = ((rows, LANES), F32)
    bonds = ((traj, mols), F32)
    own = ((owned, traj), F32)
    spread = [pltpu.VMEM((pack * mols, 2 * LANES), BF16)]
    first = call(functools.partial(first_kernel, shift), [phase, phase, packed], "first", spread, interpret)
    update = call(modes_kernel, [own, own, packed], "modes", (), interpret)
    middle = call(middle_kernel, [bonds, bonds, packed], "middle", spread, interpret)
    last = call(last_kernel, [bonds, bonds], "last", (), interpret)
    return first, update, middle, last


def exchange(packed, devices):
    blocks = packed.reshape(devices, -1, LANES)
    return lax.all_to_all(blocks, "mol", 0, 0, tiled=True).reshape(packed.shape)


def local(positions, velocities, amplitudes, momenta, sites, wavevectors, mode_freq, coupling, depth, stiffness, dipole_slope):
    devices = lax.axis_size("mol")
    traj, mols = positions.shape
    lattice = 2 * mols * devices
    first, update, middle, last = stages(traj, mols, wavevectors.shape[0], amplitudes.shape[0], 33 - lattice.bit_length())
    row = lambda x: x.reshape(1, -1)
    depth, stiffness, slope = row(depth), row(stiffness), row(dipole_slope)
    freq, coupling = row(mode_freq), row(coupling)
    high, low, partial = first(positions, slope, row(sites), wavevectors.reshape(-1, LANES // traj))
    amplitudes, momenta, weighted = update(exchange(partial, devices), amplitudes, momenta, freq, coupling)
    rows = exchange(weighted, devices)
    positions, velocities, partial = middle(rows, high, low, positions, velocities, depth, stiffness, slope)
    amplitudes, momenta, weighted = update(exchange(partial, devices), amplitudes, momenta, freq, coupling)
    rows = exchange(weighted, devices)
    positions, velocities = last(rows, high, low, positions, velocities, depth, stiffness, slope)
    return positions, velocities, amplitudes, momenta


def solution(mesh):
    both, mode, mol = P("traj", "mol"), P("mol", "traj"), P("mol")
    return jax.shard_map(
        local,
        mesh=mesh,
        in_specs=(both, both, mode, mode, mol, P(), mol, mol, mol, mol, mol),
        out_specs=(both, both, mode, mode),
        check_vma=False,
    )
```

```python
import functools

import jax
import jax.numpy as jnp
from jax import lax
from jax.experimental import pallas as pl
from jax.experimental.pallas import tpu as pltpu
from jax.sharding import PartitionSpec as P

STEP_TIME = 0.2
PLANE = 8
SINE = (25.132741928100586, -64.83582305908203, 67.0767593383789, -38.49842071533203, 14.06550407409668, -3.1933720111846924)
F32, BF16 = jnp.float32, jnp.bfloat16


def split(x):
    high = x.astype(BF16)
    return high, (x - high.astype(F32)).astype(BF16)


def both(x):
    return jnp.concatenate(split(x), axis=0)


def dot(a, b, axis):
    return lax.dot_general(a, b, (((1,), (axis,)), ((), ())), preferred_element_type=F32)


def product(halves, high, low, axis):
    traj = halves.shape[0] // 2
    first = dot(halves, high, axis)
    return first[:traj] + first[traj:] + dot(halves[:traj], low, axis)


def sine_of(residue, shift):
    turn = (residue << shift).astype(F32) * (2.0**-32)
    square = turn * turn
    value = jnp.full_like(square, SINE[-1])
    for factor in SINE[-2::-1]:
        value = value * square + factor
    return turn * (0.25 - square) * value


def advance_bonds(positions, velocities, pull, depth, stiffness, dipole_slope):
    damped = jnp.exp(-stiffness * positions)
    force = -2.0 * depth * stiffness * (1.0 - damped) * damped - dipole_slope * pull
    velocities = velocities + STEP_TIME * force
    return positions + STEP_TIME * velocities, velocities


def advance_modes(amplitudes, momenta, freq, coupling, drive):
    momenta = momenta + STEP_TIME * (-(freq * freq) * amplitudes - coupling * drive)
    return amplitudes + STEP_TIME * momenta, momenta


def start_kernel(positions, slope, sites, out_ref):
    dipole = slope[...] * positions[...]
    site = sites[...].astype(F32)
    rows = dipole.shape[0]
    for z in range(out_ref.shape[0] // (rows + 1)):
        out_ref[pl.ds(z * (rows + 1), rows), :] = dipole
        out_ref[pl.ds(z * (rows + 1) + rows, 1), :] = site


def first_kernel(shift, column, waves, amplitudes, momenta, freq, coupling, high_ref, low_ref, out_ref):
    traj, owned = amplitudes.shape
    mols = column.shape[1]
    depth = column.shape[0] // (traj + 1)
    modes = waves.shape[0]
    chunk = 4
    drive = None
    for start in range(0, depth, chunk):
        parts = []
        for z in range(start, start + chunk):
            at = z * (traj + 1)
            site = column[pl.ds(at + traj, 1), :].astype(jnp.int32)
            high, low = split(sine_of(waves[...] * site, shift))
            high_ref[:, pl.ds(z * mols, mols)] = high
            low_ref[:, pl.ds(z * mols, mols)] = low
            parts.append(both(column[pl.ds(at, traj), :]))
        columns = pl.ds(start * mols, chunk * mols)
        part = product(jnp.concatenate(parts, axis=1), high_ref[:, columns], low_ref[:, columns], 1)
        drive = part if drive is None else drive + part
    wide = lambda ref: jnp.broadcast_to(ref[...], (traj, owned))
    state = jnp.concatenate([amplitudes[...], momenta[...], wide(freq), wide(coupling)], axis=1)
    for peer in range(out_ref.shape[0]):
        out_ref[peer, :, :modes] = drive
        out_ref[peer, :, modes:] = state


def pull_blocks(weighted, high_ref, low_ref, out_ref):
    mols = out_ref.shape[2]
    pull = product(both(weighted), high_ref[...], low_ref[...], 0)
    for z in range(out_ref.shape[0]):
        out_ref[z] = pull[:, z * mols : (z + 1) * mols]


def modes_kernel(plane, high_ref, low_ref, amplitudes_out, momenta_out, freq_out, coupling_out, out_ref):
    peers = plane.shape[0]
    modes = amplitudes_out.shape[1]
    owned = modes // peers
    drive = plane[0, :, :modes]
    for peer in range(1, peers):
        drive = drive + plane[peer, :, :modes]
    whole = lambda i: jnp.concatenate(
        [plane[peer, :, modes + i * owned : modes + (i + 1) * owned] for peer in range(peers)], axis=1
    )
    freq, coupling = whole(2), whole(3)
    amplitudes, momenta = advance_modes(whole(0), whole(1), freq, coupling, drive)
    amplitudes_out[...] = amplitudes
    momenta_out[...] = momenta
    freq_out[...] = freq
    coupling_out[...] = coupling
    pull_blocks(coupling * amplitudes, high_ref, low_ref, out_ref)


def last_modes_kernel(plane, amplitudes, momenta, freq, coupling, high_ref, low_ref, amplitudes_out, momenta_out, out_ref):
    drive = plane[0]
    for peer in range(1, plane.shape[0]):
        drive = drive + plane[peer]
    new_amplitudes, new_momenta = advance_modes(amplitudes[...], momenta[...], freq[...], coupling[...], drive)
    amplitudes_out[...] = new_amplitudes
    momenta_out[...] = new_momenta
    pull_blocks(coupling[...] * new_amplitudes, high_ref, low_ref, out_ref)


def bonds_kernel(column, positions, velocities, depth, stiffness, slope, positions_out, velocities_out, *send):
    pull = column[0]
    for z in range(1, column.shape[0]):
        pull = pull + column[z]
    new_positions, new_velocities = advance_bonds(
        positions[...], velocities[...], pull, depth[...], stiffness[...], slope[...]
    )
    positions_out[...] = new_positions
    velocities_out[...] = new_velocities
    for out_ref in send:
        dipole = slope[...] * new_positions
        for z in range(out_ref.shape[0]):
            out_ref[z] = dipole


def drive_kernel(column, high_ref, low_ref, out_ref):
    dipole = jnp.concatenate([both(column[z]) for z in range(column.shape[0])], axis=1)
    drive = product(dipole, high_ref[...], low_ref[...], 1)
    for peer in range(out_ref.shape[0]):
        out_ref[peer] = drive


def call(kernel, outs, name, interpret=False):
    return pl.pallas_call(
        kernel,
        out_shape=[jax.ShapeDtypeStruct(shape, dtype) for shape, dtype in outs],
        name=name,
        interpret=interpret,
        compiler_params=None if interpret else pltpu.CompilerParams(vmem_limit_bytes=48 << 20),
    )


def stages(traj, mols, modes, owned, height, interpret=False):
    shift = 33 - (2 * mols * PLANE * height).bit_length()
    phase = ((modes, height * mols), BF16)
    bonds = ((traj, mols), F32)
    mode = ((traj, modes), F32)
    blocks = ((height, traj, mols), F32)
    made = dict(
        start=(start_kernel, [((height * (traj + 1), mols), F32)]),
        first=(functools.partial(first_kernel, shift), [phase, phase, ((PLANE, traj, modes + 4 * owned), F32)]),
        modes=(modes_kernel, [mode, mode, mode, mode, blocks]),
        bonds=(bonds_kernel, [bonds, bonds, blocks]),
        drive=(drive_kernel, [((PLANE, traj, modes), F32)]),
        last_modes=(last_modes_kernel, [mode, mode, blocks]),
        last_bonds=(bonds_kernel, [bonds, bonds]),
    )
    return {name: call(kernel, outs, name, interpret) for name, (kernel, outs) in made.items()}


def local(positions, velocities, amplitudes, momenta, sites, wavevectors, mode_freq, coupling, depth, stiffness, dipole_slope):
    height = lax.axis_size("mol") // PLANE
    traj, mols = positions.shape
    owned = amplitudes.shape[0]
    modes = PLANE * owned
    columns = [[z * PLANE + i for z in range(height)] for i in range(PLANE)]
    planes = [[z * PLANE + i for i in range(PLANE)] for z in range(height)]

    def exchange(blocks, groups):
        return lax.all_to_all(blocks, "mol", 0, 0, axis_index_groups=groups, tiled=True)

    call = stages(traj, mols, modes, owned, height)
    row = lambda x: x.reshape(1, -1)
    depth, stiffness, slope = row(depth), row(stiffness), row(dipole_slope)
    me = lax.axis_index("mol")
    waves = lax.dynamic_slice(wavevectors, (me // PLANE * modes,), (modes,)).reshape(modes, 1)

    (block,) = call["start"](positions, slope, row(sites))
    block = exchange(block.reshape(height, traj + 1, 1, mols), columns).reshape(-1, mols)
    high, low, block = call["first"](block, waves, amplitudes.T, momenta.T, row(mode_freq), row(coupling))
    *state, block = call["modes"](exchange(block, planes), high, low)
    positions, velocities, block = call["bonds"](exchange(block, columns), positions, velocities, depth, stiffness, slope)
    (block,) = call["drive"](exchange(block, columns), high, low)
    amplitudes, momenta, block = call["last_modes"](exchange(block, planes), *state, high, low)
    positions, velocities = call["last_bonds"](exchange(block, columns), positions, velocities, depth, stiffness, slope)
    mine = lambda x: lax.dynamic_slice(x, (0, me % PLANE * owned), (traj, owned)).T
    return positions, velocities, mine(amplitudes), mine(momenta)


def solution(mesh):
    bond, mode, mol = P("traj", "mol"), P("mol", "traj"), P("mol")
    return jax.shard_map(
        local,
        mesh=mesh,
        in_specs=(bond, bond, mode, mode, mol, P(), mol, mol, mol, mol, mol),
        out_specs=(bond, bond, mode, mode),
        check_vma=False,
    )
```

```python
import functools

import jax
import jax.numpy as jnp
from jax import lax
from jax.experimental import pallas as pl
from jax.experimental.pallas import tpu as pltpu
from jax.sharding import PartitionSpec as P

STEP_TIME = 0.2
PLANE = 8
LINE = 4
SINE = (25.132741928100586, -64.83582305908203, 67.0767593383789, -38.49842071533203, 14.06550407409668, -3.1933720111846924)
F32, BF16 = jnp.float32, jnp.bfloat16
SUB = 8
LANES = 128


def split(x):
    high = x.astype(BF16)
    return high, (x - high.astype(F32)).astype(BF16)


def both(x):
    return jnp.concatenate(split(x), axis=0)


def dot(a, b, axis):
    return lax.dot_general(a, b, (((1,), (axis,)), ((), ())), preferred_element_type=F32)


def product(halves, high, low, axis):
    traj = halves.shape[0] // 2
    first = dot(halves, high, axis)
    return first[:traj] + first[traj:] + dot(halves[:traj], low, axis)


def sine_of(residue, shift):
    turn = (residue << shift).astype(F32) * (2.0**-32)
    square = turn * turn
    value = jnp.full_like(square, SINE[-1])
    for factor in SINE[-2::-1]:
        value = value * square + factor
    return turn * (0.25 - square) * value


def morse(positions, depth, stiffness):
    damped = jnp.exp(-stiffness * positions)
    return -2.0 * depth * stiffness * (1.0 - damped) * damped


def advance_modes(amplitudes, momenta, freq, coupling, drive):
    momenta = momenta + STEP_TIME * (-(freq * freq) * amplitudes - coupling * drive)
    return amplitudes + STEP_TIME * momenta, momenta


def sum_over(ref, part=()):
    total = ref[(0, *part)]
    for i in range(1, ref.shape[0]):
        total = total + ref[(i, *part)]
    return total


def block_rows(traj):
    return 3 * traj + 3 - traj // 2


def start_kernel(positions, velocities, slope, sites, depth, stiffness, amplitudes, momenta, freq, coupling,
                 out_ref, free_positions, free_velocities, bond_ref, *scratch):
    hbm = (positions, velocities, slope, sites, depth, stiffness, amplitudes, momenta, freq, coupling)
    held, sems = scratch[:-1], scratch[-1]
    copies = [pltpu.make_async_copy(a, b, sems.at[i]) for i, (a, b) in enumerate(zip(hbm, held))]
    for copy in copies:
        copy.start()
    for copy in copies:
        copy.wait()
    positions, velocities, slope, sites, depth, stiffness, amplitudes, momenta, freq, coupling = (ref[...] for ref in held)
    traj, owned = amplitudes.shape
    half = traj // 2
    speed = velocities + STEP_TIME * morse(positions, depth, stiffness)
    moved = positions + STEP_TIME * speed
    free_positions[...] = moved
    free_velocities[...] = speed
    bond_ref[...] = jnp.concatenate([slope, depth, stiffness, jnp.zeros((SUB - 3, LANES), F32)], axis=0)
    modes = jnp.concatenate([amplitudes[:half], momenta[:half], amplitudes[half:], momenta[half:]], axis=1)
    own = jnp.concatenate([coupling, freq, coupling, freq], axis=1)
    rows = block_rows(traj)
    for z in range(out_ref.shape[0] // rows):
        at = z * rows
        for piece in (slope * positions, slope * moved, slope, sites.astype(F32), modes, own):
            out_ref[pl.ds(at, piece.shape[0]), :] = piece
            at += piece.shape[0]


def first_kernel(shift, traj, place, column, waves, high_ref, low_ref, free_ref, square_ref, out_ref, site_ref, dipole_ref):
    rows = block_rows(traj)
    half = traj // 2
    height = column.shape[0] // rows
    modes = waves.shape[0]
    chunk = modes // LINE
    for z in range(height):
        at = z * rows
        columns = pl.ds(z * LANES, LANES)
        dipole_ref[:, columns] = both(column[pl.ds(at, traj), :])
        free_ref[:, columns] = column[pl.ds(at + traj, traj), :]
        slope = column[pl.ds(at + 2 * traj, 1), :]
        square_ref[:, columns] = (STEP_TIME * STEP_TIME) * slope * slope
        site_ref[z] = column[pl.ds(at + 2 * traj + 1, 1), :].astype(jnp.int32)

    def fill(z, carry):
        columns = pl.ds(pl.multiple_of(z * LANES, LANES), LANES)
        site = site_ref[z]
        for part in range(LINE):
            taken = pl.ds(part * chunk, chunk)
            high, low = split(sine_of(waves[taken, :] * site, shift))
            high_ref[taken, columns] = high
            low_ref[taken, columns] = low
        return carry

    lax.fori_loop(0, height, fill, 0)
    drive = product(dipole_ref[...], high_ref[...], low_ref[...], 1)
    state = []
    own = []
    for quad in range(height // LINE):
        block = jnp.zeros((half + 1, LANES), F32)
        for i in range(LINE):
            at = (quad * LINE + i) * rows + 2 * traj + 2
            block = jnp.where(place[0] == i, column[pl.ds(at, half + 1), :], block)
        state.append(block[:half])
        own.append(block[half:])
    tail = jnp.concatenate(state + own + [jnp.zeros((SUB - len(own), LANES), F32)], axis=0)
    for peer in range(out_ref.shape[0]):
        for tile in range(modes // LANES):
            out_ref[peer, pl.ds(tile * traj, traj), :] = drive[:, tile * LANES : (tile + 1) * LANES]
        out_ref[peer, pl.ds(modes // LANES * traj, tail.shape[0]), :] = tail


def modes_kernel(owned, plane, high_ref, low_ref, amplitudes_out, momenta_out, freq_out, coupling_out, out_ref):
    traj, modes = amplitudes_out.shape
    half = traj // 2
    quads = modes // (PLANE * owned)
    base = modes // LANES * traj
    drive = jnp.concatenate(
        [sum_over(plane, (pl.ds(tile * traj, traj),)) for tile in range(modes // LANES)], axis=1
    )

    def gather(row, count, lane):
        return jnp.concatenate(
            [
                plane[peer, pl.ds(row(quad), count), lane * owned : (lane + 1) * owned]
                for quad in range(quads)
                for peer in range(PLANE)
            ],
            axis=1,
        )

    state = lambda quad: base + quad * half
    own = lambda quad: base + quads * half + quad
    amplitudes = jnp.concatenate([gather(state, half, 0), gather(state, half, 2)], axis=0)
    momenta = jnp.concatenate([gather(state, half, 1), gather(state, half, 3)], axis=0)
    coupling, freq = gather(own, 1, 0), gather(own, 1, 1)
    amplitudes, momenta = advance_modes(amplitudes, momenta, freq, coupling, drive)
    amplitudes_out[...] = amplitudes
    momenta_out[...] = momenta
    freq_out[...] = freq
    coupling_out[...] = coupling
    pull = product(both(coupling * amplitudes), high_ref[...], low_ref[...], 0)
    for peer in range(out_ref.shape[0]):
        for z in range(out_ref.shape[1] // traj):
            out_ref[peer, pl.ds(z * traj, traj), :] = pull[:, z * LANES : (z + 1) * LANES]


def middle_kernel(place, line, free_ref, square_ref, high_ref, low_ref, pull_out, out_ref):
    traj = pull_out.shape[0]
    own = jnp.zeros(pull_out.shape, F32)
    parts = []
    for z in range(line.shape[1] // traj):
        columns = pl.ds(z * LANES, LANES)
        pull = sum_over(line, (pl.ds(z * traj, traj),))
        own = jnp.where(place[1] == z, pull, own)
        parts.append(both(free_ref[:, columns] - square_ref[:, columns] * pull))
    pull_out[...] = own
    drive = product(jnp.concatenate(parts, axis=1), high_ref[...], low_ref[...], 1)
    for peer in range(out_ref.shape[0]):
        for tile in range(drive.shape[1] // LANES):
            out_ref[peer, pl.ds(tile * traj, traj), :] = drive[:, tile * LANES : (tile + 1) * LANES]


def last_modes_kernel(place, plane, amplitudes, momenta, freq, coupling, high_ref, low_ref, amplitudes_out, momenta_out, out_ref):
    traj, modes = amplitudes.shape
    drive = jnp.concatenate(
        [sum_over(plane, (pl.ds(tile * traj, traj),)) for tile in range(modes // LANES)], axis=1
    )
    new_amplitudes, new_momenta = advance_modes(amplitudes[...], momenta[...], freq[...], coupling[...], drive)
    amplitudes_out[...] = new_amplitudes
    momenta_out[...] = new_momenta
    width = LINE * LANES
    columns = pl.ds(pl.multiple_of(place[2] * width, width), width)
    pull = product(both(coupling[...] * new_amplitudes), high_ref[:, columns], low_ref[:, columns], 0)
    for i in range(LINE):
        out_ref[i] = pull[:, i * LANES : (i + 1) * LANES]


def last_kernel(line, pull, free_positions, free_velocities, bond_ref, positions_out, velocities_out):
    slope, depth, stiffness = (bond_ref[i : i + 1, :] for i in range(3))
    velocities = free_velocities[...] - STEP_TIME * (slope * pull[...])
    positions = free_positions[...] - STEP_TIME * (STEP_TIME * (slope * pull[...]))
    velocities = velocities + STEP_TIME * (morse(positions, depth, stiffness) - slope * sum_over(line))
    velocities_out[...] = velocities
    positions_out[...] = positions + STEP_TIME * velocities


def call(kernel, outs, name, scratch=(), places=False, inputs=None, interpret=False):
    def run(*args):
        vmem = pl.BlockSpec(memory_space=pltpu.VMEM)
        first = [pl.BlockSpec(memory_space=pltpu.SMEM)] if places else []
        specs = first + [vmem if inputs is None else pl.BlockSpec(memory_space=inputs)] * (len(args) - len(first))
        return pl.pallas_call(
            kernel,
            out_shape=[jax.ShapeDtypeStruct(shape, dtype) for shape, dtype in outs],
            in_specs=specs,
            out_specs=[vmem] * len(outs),
            scratch_shapes=list(scratch),
            name=name,
            interpret=interpret,
            compiler_params=None if interpret else pltpu.CompilerParams(vmem_limit_bytes=56 << 20),
        )(*args)

    return run


def stages(traj, mols, owned, height, interpret=False):
    modes = height // LINE * PLANE * owned
    lattice = 2 * mols * PLANE * height
    shift = 33 - lattice.bit_length()
    rows = block_rows(traj)
    here = height * mols
    tail = (height // LINE) * traj // 2 + SUB
    bond, row, mode, mode_row = (traj, mols), (1, mols), (traj, modes), (1, modes)
    own, own_row = (traj, owned), (1, owned)
    f = lambda *shape: (shape, F32)
    held = [pltpu.VMEM(s, F32) for s in (bond, bond, row)] + [pltpu.VMEM(row, jnp.int32)]
    held += [pltpu.VMEM(s, F32) for s in (row, row, own, own, own_row, own_row)]
    phase = ((modes, here), BF16)
    sent = modes // LANES * traj
    make = functools.partial(call, interpret=interpret)
    return dict(
        start=make(start_kernel, [f(height * rows, LANES), f(*bond), f(*bond), f(SUB, mols)], "start",
                   held + [pltpu.SemaphoreType.DMA((len(held),))], inputs=pl.ANY),
        first=make(functools.partial(first_kernel, shift, traj),
                   [phase, phase, f(traj, here), f(1, here), f(PLANE, sent + tail, LANES)], "first",
                   [pltpu.VMEM((height, 1, LANES), jnp.int32), pltpu.VMEM((2 * traj, here), BF16)], places=True),
        modes=make(functools.partial(modes_kernel, owned),
                   [f(*mode), f(*mode), f(*mode_row), f(*mode_row), f(LINE, height * traj, LANES)], "modes"),
        middle=make(middle_kernel, [f(*bond), f(PLANE, sent, LANES)], "middle", places=True),
        last_modes=make(last_modes_kernel, [f(*mode), f(*mode), f(LINE, traj, LANES)], "last_modes", places=True),
        last=make(last_kernel, [f(*bond), f(*bond)], "last"),
    )


def local(positions, velocities, amplitudes, momenta, sites, wavevectors, mode_freq, coupling, depth, stiffness, dipole_slope):
    height = lax.axis_size("mol") // PLANE
    traj, mols = positions.shape
    owned = amplitudes.shape[0]
    quads = height // LINE
    columns = [[z * PLANE + i for z in range(height)] for i in range(PLANE)]
    planes = [[z * PLANE + i for i in range(PLANE)] for z in range(height)]
    lines = [[(q * LINE + j) * PLANE + i for j in range(LINE)] for q in range(quads) for i in range(PLANE)]

    def exchange(blocks, groups):
        return lax.all_to_all(blocks, "mol", 0, 0, axis_index_groups=groups, tiled=True)

    run = stages(traj, mols, owned, height)
    row = lambda x: x.reshape(1, -1)
    me = lax.axis_index("mol")
    z, peer = me // PLANE, me % PLANE
    place = jnp.stack([z % LINE, z, z // LINE]).astype(jnp.int32)
    waves = lax.dynamic_slice(
        wavevectors.reshape(quads, -1), (0, z % LINE * PLANE * owned), (quads, PLANE * owned)
    ).reshape(-1, 1)

    block, free_positions, free_velocities, bond = run["start"](
        positions, velocities, row(dipole_slope), row(sites), row(depth), row(stiffness), amplitudes.T, momenta.T, row(mode_freq), row(coupling)
    )
    block = exchange(block.reshape(height, -1, 1, mols), columns).reshape(-1, mols)
    high, low, free, square, block = run["first"](place, block, waves)
    *state, block = run["modes"](exchange(block, planes), high, low)
    pull, block = run["middle"](place, exchange(block, lines), free, square, high, low)
    amplitudes, momenta, block = run["last_modes"](place, exchange(block, planes), *state, high, low)
    positions, velocities = run["last"](exchange(block, lines), pull, free_positions, free_velocities, bond)
    mine = lambda x: lax.dynamic_slice(x, (0, (z // LINE * PLANE + peer) * owned), (traj, owned)).T
    return positions, velocities, mine(amplitudes), mine(momenta)


def solution(mesh):
    bond, mode, mol = P("traj", "mol"), P("mol", "traj"), P("mol")
    return jax.shard_map(
        local,
        mesh=mesh,
        in_specs=(bond, bond, mode, mode, mol, P(), mol, mol, mol, mol, mol),
        out_specs=(bond, bond, mode, mode),
        check_vma=False,
    )
```

```python
import functools

import jax
import jax.numpy as jnp
from jax import lax
from jax.experimental import pallas as pl
from jax.experimental.pallas import tpu as pltpu
from jax.sharding import PartitionSpec as P

STEP_TIME = 0.2
SET = 16
SINE = (25.132741928100586, -64.83582305908203, 67.0767593383789, -38.49842071533203, 14.06550407409668, -3.1933720111846924)
F32, BF16 = jnp.float32, jnp.bfloat16
SUB = 8
LANES = 128


def split(x):
    high = x.astype(BF16)
    return high, (x - high.astype(F32)).astype(BF16)


def both(x):
    return jnp.concatenate(split(x), axis=0)


def dot(a, b, axis):
    return lax.dot_general(a, b, (((1,), (axis,)), ((), ())), preferred_element_type=F32)


def product(halves, high, low, axis):
    traj = halves.shape[0] // 2
    first = dot(halves, high, axis)
    return first[:traj] + first[traj:] + dot(halves[:traj], low, axis)


def sine_of(residue, shift):
    turn = (residue << shift).astype(F32) * (2.0**-32)
    square = turn * turn
    value = jnp.full_like(square, SINE[-1])
    for factor in SINE[-2::-1]:
        value = value * square + factor
    return turn * (0.25 - square) * value


def morse(positions, depth, stiffness):
    damped = jnp.exp(-stiffness * positions)
    return -2.0 * depth * stiffness * (1.0 - damped) * damped


def sum_over(ref, part=()):
    total = ref[(0, *part)]
    for i in range(1, ref.shape[0]):
        total = total + ref[(i, *part)]
    return total


def block_rows(traj):
    return 3 * traj + 3 - traj // 2


def start_kernel(positions, velocities, slope, sites, depth, stiffness, amplitudes, momenta, freq, coupling,
                 out_ref, free_positions, free_velocities, bond_ref, *scratch):
    hbm = (positions, velocities, slope, sites, depth, stiffness, amplitudes, momenta, freq, coupling)
    held, sems = scratch[:-1], scratch[-1]
    copies = [pltpu.make_async_copy(a, b, sems.at[i]) for i, (a, b) in enumerate(zip(hbm, held))]
    for copy in copies:
        copy.start()
    for copy in copies:
        copy.wait()
    positions, velocities, slope, sites, depth, stiffness, amplitudes, momenta, freq, coupling = (ref[...] for ref in held)
    traj, owned = amplitudes.shape
    half = traj // 2
    speed = velocities + STEP_TIME * morse(positions, depth, stiffness)
    moved = positions + STEP_TIME * speed
    free_positions[...] = moved
    free_velocities[...] = speed
    bond_ref[...] = jnp.concatenate([slope, depth, stiffness, jnp.zeros((SUB - 3, LANES), F32)], axis=0)
    modes = jnp.concatenate([amplitudes[:half], momenta[:half], amplitudes[half:], momenta[half:]], axis=1)
    own = jnp.concatenate([coupling, freq, coupling, freq], axis=1)
    rows = block_rows(traj)
    for block in range(out_ref.shape[0] // rows):
        at = block * rows
        for piece in (slope * positions, slope * moved, slope, sites.astype(F32), modes, own):
            out_ref[pl.ds(at, piece.shape[0]), :] = piece
            at += piece.shape[0]


def first_kernel(shift, traj, place, column, waves, high_ref, low_ref, free_ref, square_ref, amplitudes_ref, momenta_ref,
                 own_ref, place_out, out_ref, dipole_ref):
    place_out[0] = place[0]
    rows = block_rows(traj)
    half = traj // 2
    sets = column.shape[0] // rows
    chunk = out_ref.shape[2]
    owned = chunk // sets
    sites = []
    for q in range(sets):
        at = q * rows
        columns = pl.ds(q * LANES, LANES)
        dipole_ref[:, columns] = both(column[pl.ds(at, traj), :])
        free_ref[:, columns] = column[pl.ds(at + traj, traj), :]
        slope = column[pl.ds(at + 2 * traj, 1), :]
        square_ref[:, columns] = (STEP_TIME * STEP_TIME) * slope * slope
        sites.append(column[pl.ds(at + 2 * traj + 1, 1), :].astype(jnp.int32))

    def gather(row, count, lane):
        return jnp.concatenate(
            [column[pl.ds(q * rows + row, count), lane * owned : (lane + 1) * owned] for q in range(sets)], axis=1
        )

    at = 2 * traj + 2
    amplitudes_ref[...] = jnp.concatenate([gather(at, half, 0), gather(at, half, 2)], axis=0)
    momenta_ref[...] = jnp.concatenate([gather(at, half, 1), gather(at, half, 3)], axis=0)
    own_ref[...] = jnp.concatenate([gather(at + half, 1, 0), gather(at + half, 1, 1)], axis=0)

    def fill(member, carry):
        taken = pl.ds(pl.multiple_of(member * chunk, chunk), chunk)
        wave = waves[taken, :]
        drive = None
        parts = 2
        for part in range(parts):
            for q in range(part * sets // parts, (part + 1) * sets // parts):
                columns = pl.ds(q * LANES, LANES)
                high, low = split(sine_of(wave * sites[q], shift))
                high_ref[taken, columns] = high
                low_ref[taken, columns] = low
            columns = pl.ds(part * sets // parts * LANES, sets // parts * LANES)
            piece = product(dipole_ref[:, columns], high_ref[taken, columns], low_ref[taken, columns], 1)
            drive = piece if drive is None else drive + piece
        out_ref[member] = drive
        return carry

    lax.fori_loop(0, out_ref.shape[0], fill, 0)


def modes_kernel(received, amplitudes, momenta, own, amplitudes_out, momenta_out, out_ref):
    drive = sum_over(received)
    coupling, freq = own[0:1, :], own[1:2, :]
    new_momenta = momenta[...] + STEP_TIME * (-(freq * freq) * amplitudes[...] - coupling * drive)
    new_amplitudes = amplitudes[...] + STEP_TIME * new_momenta
    momenta_out[...] = new_momenta
    amplitudes_out[...] = new_amplitudes
    weighted = coupling * new_amplitudes
    for member in range(out_ref.shape[0]):
        out_ref[member] = weighted


def pull_of(received, high_ref, low_ref, columns):
    chunk = received.shape[2]
    pull = None
    for member in range(received.shape[0]):
        rows = pl.ds(member * chunk, chunk)
        piece = product(both(received[member]), high_ref[rows, columns], low_ref[rows, columns], 0)
        pull = piece if pull is None else pull + piece
    return pull


def middle_kernel(place, received, free_ref, square_ref, high_ref, low_ref, pull_out, out_ref):
    pull = pull_of(received, high_ref, low_ref, slice(None))
    own = pull[:, :LANES]
    for q in range(1, pull.shape[1] // LANES):
        own = jnp.where(place[0] == q, pull[:, q * LANES : (q + 1) * LANES], own)
    pull_out[...] = own
    dipole = both(free_ref[...] - square_ref[...] * pull)
    chunk = out_ref.shape[2]
    for member in range(out_ref.shape[0]):
        rows = pl.ds(member * chunk, chunk)
        out_ref[member] = product(dipole, high_ref[rows, :], low_ref[rows, :], 1)


def last_kernel(place, received, high_ref, low_ref, pull, free_positions, free_velocities, bond_ref, amplitudes, momenta,
                positions_out, velocities_out, amplitudes_out, momenta_out):
    owned = amplitudes_out.shape[1]
    for whole, own in ((amplitudes, amplitudes_out), (momenta, momenta_out)):
        mine = whole[:, :owned]
        for q in range(1, whole.shape[1] // owned):
            mine = jnp.where(place[0] == q, whole[:, q * owned : (q + 1) * owned], mine)
        own[...] = mine
    columns = pl.ds(pl.multiple_of(place[0] * LANES, LANES), LANES)
    last_pull = pull_of(received, high_ref, low_ref, columns)
    slope, depth, stiffness = (bond_ref[i : i + 1, :] for i in range(3))
    first = slope * pull[...]
    velocities = free_velocities[...] - STEP_TIME * first
    positions = free_positions[...] - STEP_TIME * (STEP_TIME * first)
    velocities = velocities + STEP_TIME * (morse(positions, depth, stiffness) - slope * last_pull)
    velocities_out[...] = velocities
    positions_out[...] = positions + STEP_TIME * velocities


def call(kernel, outs, name, spaces, scratch=(), grant=20, interpret=False):
    kinds = {"V": pltpu.VMEM, "S": pltpu.SMEM, "H": pltpu.HBM}
    return pl.pallas_call(
        kernel,
        out_shape=[jax.ShapeDtypeStruct(shape, dtype) for shape, dtype in outs],
        in_specs=[pl.BlockSpec(memory_space=kinds[letter]) for letter in spaces],
        out_specs=[pl.BlockSpec(memory_space=kinds["S" if dtype == jnp.int32 else "V"]) for _, dtype in outs],
        scratch_shapes=list(scratch),
        name=name,
        interpret=interpret,
        compiler_params=None if interpret else pltpu.CompilerParams(vmem_limit_bytes=grant << 20),
    )


def stages(traj, mols, owned, sets, interpret=False):
    lattice = 2 * mols * SET * sets
    shift = 33 - lattice.bit_length()
    modes, chunk, here = sets * SET * owned, sets * owned, sets * mols
    bond, row, own, own_row = (traj, mols), (1, mols), (traj, owned), (1, owned)
    f = lambda *shape: (shape, F32)
    held = [pltpu.VMEM(s, F32) for s in (bond, bond, row)] + [pltpu.VMEM(row, jnp.int32)]
    held += [pltpu.VMEM(s, F32) for s in (row, row, own, own, own_row, own_row)]
    phase = ((modes, here), BF16)
    state, blocks = f(traj, chunk), f(SET, traj, chunk)
    make = functools.partial(call, interpret=interpret)
    return dict(
        start=make(start_kernel, [f(sets * block_rows(traj), LANES), f(*bond), f(*bond), f(SUB, mols)], "start", 10 * "H",
                   held + [pltpu.SemaphoreType.DMA((len(held),))], grant=56),
        first=make(functools.partial(first_kernel, shift, traj),
                   [phase, phase, f(traj, here), f(1, here), state, state, f(2, chunk), ((1,), jnp.int32), blocks], "first", "SVV",
                   [pltpu.VMEM((2 * traj, here), BF16)]),
        modes=make(modes_kernel, [state, state, blocks], "modes", "VVVV"),
        middle=make(middle_kernel, [f(*bond), blocks], "middle", "SVVVVV"),
        last=make(last_kernel, [f(*bond), f(*bond), f(*own), f(*own)], "last", "S" + 9 * "V"),
    )


def local(positions, velocities, amplitudes, momenta, sites, wavevectors, mode_freq, coupling, depth, stiffness, dipole_slope):
    sets = lax.axis_size("mol") // SET
    traj, mols = positions.shape
    owned = amplitudes.shape[0]
    across = [[q * SET + i for q in range(sets)] for i in range(SET)]
    inside = [[q * SET + i for i in range(SET)] for q in range(sets)]

    def exchange(blocks, groups):
        return lax.all_to_all(blocks, "mol", 0, 0, axis_index_groups=groups, tiled=True)

    run = stages(traj, mols, owned, sets)
    row = lambda x: x.reshape(1, -1)
    place = (lax.axis_index("mol") // SET).astype(jnp.int32).reshape(1)
    waves = wavevectors.reshape(sets, SET, owned).transpose(1, 0, 2).reshape(-1, 1)

    block, free_positions, free_velocities, bond = run["start"](
        positions, velocities, row(dipole_slope), row(sites), row(depth), row(stiffness), amplitudes.T, momenta.T, row(mode_freq), row(coupling)
    )
    block = exchange(block.reshape(sets, -1, 1, mols), across).reshape(-1, mols)
    high, low, free, square, amplitudes, momenta, own, place, block = run["first"](place, block, waves)
    amplitudes, momenta, block = run["modes"](exchange(block, inside), amplitudes, momenta, own)
    pull, block = run["middle"](place, exchange(block, inside), free, square, high, low)
    amplitudes, momenta, block = run["modes"](exchange(block, inside), amplitudes, momenta, own)
    positions, velocities, amplitudes, momenta = run["last"](
        place, exchange(block, inside), high, low, pull, free_positions, free_velocities, bond, amplitudes, momenta
    )
    return positions, velocities, amplitudes.T, momenta.T


def solution(mesh):
    bond, mode, mol = P("traj", "mol"), P("mol", "traj"), P("mol")
    return jax.shard_map(
        local,
        mesh=mesh,
        in_specs=(bond, bond, mode, mode, mol, P(), mol, mol, mol, mol, mol),
        out_specs=(bond, bond, mode, mode),
        check_vma=False,
    )
```

```python
import functools

import jax
import jax.numpy as jnp
from jax import lax
from jax.experimental import pallas as pl
from jax.experimental.pallas import tpu as pltpu
from jax.sharding import PartitionSpec as P

STEP_TIME = 0.2
SET = 16
SINE = (25.13273048400879, -64.83467864990234, 67.04389953613281, -38.12319564819336, 12.233302116394043)
F32, BF16 = jnp.float32, jnp.bfloat16
SUB = 8
LANES = 128


def split(x):
    high = x.astype(BF16)
    return high, (x - high.astype(F32)).astype(BF16)


def both(x):
    return jnp.concatenate(split(x), axis=0)


def dot(a, b, axis):
    return lax.dot_general(a, b, (((1,), (axis,)), ((), ())), preferred_element_type=F32)


def product(halves, high, low, axis):
    traj = halves.shape[0] // 2
    first = dot(halves, high, axis)
    return first[:traj] + first[traj:] + dot(halves[:traj], low, axis)


def sine_of(product):
    turn = product.astype(F32) * (2.0**-32)
    square = turn * turn
    value = square * SINE[-1] + SINE[-2]
    for factor in SINE[-3::-1]:
        value = value * square + factor
    return turn * (0.25 - square) * value


def morse(positions, depth, stiffness):
    damped = jnp.exp(-stiffness * positions)
    return -2.0 * depth * stiffness * (1.0 - damped) * damped


def sum_over(ref, part=()):
    total = ref[(0, *part)]
    for i in range(1, ref.shape[0]):
        total = total + ref[(i, *part)]
    return total


def block_rows(traj):
    return 3 * traj + 3 - traj // 2


def start_kernel(positions, velocities, slope, sites, depth, stiffness, amplitudes, momenta, freq, coupling,
                 out_ref, free_positions, free_velocities, bond_ref, *scratch):
    hbm = (positions, velocities, slope, sites, depth, stiffness, amplitudes, momenta, freq, coupling)
    held, sems = scratch[:-1], scratch[-1]
    copies = [pltpu.make_async_copy(a, b, sems.at[i]) for i, (a, b) in enumerate(zip(hbm, held))]
    for copy in copies:
        copy.start()
    for copy in copies:
        copy.wait()
    positions, velocities, slope, sites, depth, stiffness, amplitudes, momenta, freq, coupling = (ref[...] for ref in held)
    traj, owned = amplitudes.shape
    half = traj // 2
    speed = velocities + STEP_TIME * morse(positions, depth, stiffness)
    moved = positions + STEP_TIME * speed
    free_positions[...] = moved
    free_velocities[...] = speed
    bond_ref[...] = jnp.concatenate([slope, depth, stiffness, jnp.zeros((SUB - 3, LANES), F32)], axis=0)
    modes = jnp.concatenate([amplitudes[:half], momenta[:half], amplitudes[half:], momenta[half:]], axis=1)
    own = jnp.concatenate([coupling, freq, coupling, freq], axis=1)
    rows = block_rows(traj)
    for block in range(out_ref.shape[0] // rows):
        at = block * rows
        for piece in (slope * positions, slope * moved, slope, sites.astype(F32), modes, own):
            out_ref[pl.ds(at, piece.shape[0]), :] = piece
            at += piece.shape[0]


def first_kernel(shift, traj, place, column, waves, high_ref, low_ref, free_ref, square_ref, amplitudes_ref, momenta_ref,
                 own_ref, place_out, out_ref, dipole_ref, held_high, held_low):
    place_out[0] = place[0]
    rows = block_rows(traj)
    half = traj // 2
    sets = column.shape[0] // rows
    chunk = out_ref.shape[2]
    owned = chunk // sets
    sites = []
    for q in range(sets):
        at = q * rows
        columns = pl.ds(q * LANES, LANES)
        dipole_ref[:, columns] = both(column[pl.ds(at, traj), :])
        free_ref[:, columns] = column[pl.ds(at + traj, traj), :]
        slope = column[pl.ds(at + 2 * traj, 1), :]
        square_ref[:, columns] = (STEP_TIME * STEP_TIME) * slope * slope
        sites.append(column[pl.ds(at + 2 * traj + 1, 1), :].astype(jnp.int32) << shift)

    def gather(row, count, lane):
        return jnp.concatenate(
            [column[pl.ds(q * rows + row, count), lane * owned : (lane + 1) * owned] for q in range(sets)], axis=1
        )

    at = 2 * traj + 2
    amplitudes_ref[...] = jnp.concatenate([gather(at, half, 0), gather(at, half, 2)], axis=0)
    momenta_ref[...] = jnp.concatenate([gather(at, half, 1), gather(at, half, 3)], axis=0)
    own_ref[...] = jnp.concatenate([gather(at + half, 1, 0), gather(at + half, 1, 1)], axis=0)

    def fill(member, slot):
        taken = pl.ds(pl.multiple_of(member * chunk, chunk), chunk)
        wave = waves[taken, :]
        for q in range(sets):
            columns = pl.ds(q * LANES, LANES)
            high, low = split(sine_of(wave * sites[q]))
            high_ref[taken, columns] = high
            low_ref[taken, columns] = low
            held_high[slot, :, columns] = high
            held_low[slot, :, columns] = low

    def finish(member, slot):
        out_ref[member] = product(dipole_ref[...], held_high[slot], held_low[slot], 1)

    def step(pair, carry):
        for slot in range(2):
            finish(2 * pair + slot, slot)
            fill(2 * pair + slot + 1, 1 - slot)
        return carry

    members = out_ref.shape[0]
    fill(0, 0)
    lax.fori_loop(0, members // 2 - 1, step, 0)
    finish(members - 2, 0)
    fill(members - 1, 1)
    finish(members - 1, 1)


def modes_kernel(received, amplitudes, momenta, own, amplitudes_out, momenta_out, out_ref):
    drive = sum_over(received)
    coupling, freq = own[0:1, :], own[1:2, :]
    new_momenta = momenta[...] + STEP_TIME * (-(freq * freq) * amplitudes[...] - coupling * drive)
    new_amplitudes = amplitudes[...] + STEP_TIME * new_momenta
    momenta_out[...] = new_momenta
    amplitudes_out[...] = new_amplitudes
    weighted = coupling * new_amplitudes
    for member in range(out_ref.shape[0]):
        out_ref[member] = weighted


def pull_of(received, high_ref, low_ref, columns):
    chunk = received.shape[2]
    pull = None
    for member in range(received.shape[0]):
        rows = pl.ds(member * chunk, chunk)
        piece = product(both(received[member]), high_ref[rows, columns], low_ref[rows, columns], 0)
        pull = piece if pull is None else pull + piece
    return pull


def middle_kernel(place, received, free_ref, square_ref, high_ref, low_ref, pull_out, out_ref):
    pull = pull_of(received, high_ref, low_ref, slice(None))
    own = pull[:, :LANES]
    for q in range(1, pull.shape[1] // LANES):
        own = jnp.where(place[0] == q, pull[:, q * LANES : (q + 1) * LANES], own)
    pull_out[...] = own
    dipole = both(free_ref[...] - square_ref[...] * pull)
    chunk = out_ref.shape[2]
    for member in range(out_ref.shape[0]):
        rows = pl.ds(member * chunk, chunk)
        out_ref[member] = product(dipole, high_ref[rows, :], low_ref[rows, :], 1)


def last_kernel(place, received, high_ref, low_ref, pull, free_positions, free_velocities, bond_ref, amplitudes, momenta,
                positions_out, velocities_out, amplitudes_out, momenta_out):
    owned = amplitudes_out.shape[1]
    for whole, own in ((amplitudes, amplitudes_out), (momenta, momenta_out)):
        mine = whole[:, :owned]
        for q in range(1, whole.shape[1] // owned):
            mine = jnp.where(place[0] == q, whole[:, q * owned : (q + 1) * owned], mine)
        own[...] = mine
    columns = pl.ds(pl.multiple_of(place[0] * LANES, LANES), LANES)
    last_pull = pull_of(received, high_ref, low_ref, columns)
    slope, depth, stiffness = (bond_ref[i : i + 1, :] for i in range(3))
    first = slope * pull[...]
    velocities = free_velocities[...] - STEP_TIME * first
    positions = free_positions[...] - STEP_TIME * (STEP_TIME * first)
    velocities = velocities + STEP_TIME * (morse(positions, depth, stiffness) - slope * last_pull)
    velocities_out[...] = velocities
    positions_out[...] = positions + STEP_TIME * velocities


def call(kernel, outs, name, spaces, scratch=(), grant=20, interpret=False):
    kinds = {"V": pltpu.VMEM, "S": pltpu.SMEM, "H": pltpu.HBM}
    return pl.pallas_call(
        kernel,
        out_shape=[jax.ShapeDtypeStruct(shape, dtype) for shape, dtype in outs],
        in_specs=[pl.BlockSpec(memory_space=kinds[letter]) for letter in spaces],
        out_specs=[pl.BlockSpec(memory_space=kinds["S" if dtype == jnp.int32 else "V"]) for _, dtype in outs],
        scratch_shapes=list(scratch),
        name=name,
        interpret=interpret,
        compiler_params=None if interpret else pltpu.CompilerParams(vmem_limit_bytes=grant << 20),
    )


def stages(traj, mols, owned, sets, interpret=False):
    lattice = 2 * mols * SET * sets
    shift = 33 - lattice.bit_length()
    modes, chunk, here = sets * SET * owned, sets * owned, sets * mols
    bond, row, own, own_row = (traj, mols), (1, mols), (traj, owned), (1, owned)
    f = lambda *shape: (shape, F32)
    held = [pltpu.VMEM(s, F32) for s in (bond, bond, row)] + [pltpu.VMEM(row, jnp.int32)]
    held += [pltpu.VMEM(s, F32) for s in (row, row, own, own, own_row, own_row)]
    phase = ((modes, here), BF16)
    state, blocks = f(traj, chunk), f(SET, traj, chunk)
    make = functools.partial(call, interpret=interpret)
    return dict(
        start=make(start_kernel, [f(sets * block_rows(traj), LANES), f(*bond), f(*bond), f(SUB, mols)], "start", 10 * "H",
                   held + [pltpu.SemaphoreType.DMA((len(held),))], grant=56),
        first=make(functools.partial(first_kernel, shift, traj),
                   [phase, phase, f(traj, here), f(1, here), state, state, f(2, chunk), ((1,), jnp.int32), blocks], "first", "SVV",
                   [pltpu.VMEM((2 * traj, here), BF16)] + 2 * [pltpu.VMEM((2, chunk, here), BF16)]),
        modes=make(modes_kernel, [state, state, blocks], "modes", "VVVV"),
        middle=make(middle_kernel, [f(*bond), blocks], "middle", "SVVVVV"),
        last=make(last_kernel, [f(*bond), f(*bond), f(*own), f(*own)], "last", "S" + 9 * "V"),
    )


def local(positions, velocities, amplitudes, momenta, sites, wavevectors, mode_freq, coupling, depth, stiffness, dipole_slope):
    sets = lax.axis_size("mol") // SET
    traj, mols = positions.shape
    owned = amplitudes.shape[0]
    across = [[q * SET + i for q in range(sets)] for i in range(SET)]
    inside = [[q * SET + i for i in range(SET)] for q in range(sets)]

    def exchange(blocks, groups):
        return lax.all_to_all(blocks, "mol", 0, 0, axis_index_groups=groups, tiled=True)

    run = stages(traj, mols, owned, sets)
    row = lambda x: x.reshape(1, -1)
    place = (lax.axis_index("mol") // SET).astype(jnp.int32).reshape(1)
    waves = wavevectors.reshape(sets, SET, owned).transpose(1, 0, 2).reshape(-1, 1)

    block, free_positions, free_velocities, bond = run["start"](
        positions, velocities, row(dipole_slope), row(sites), row(depth), row(stiffness), amplitudes.T, momenta.T, row(mode_freq), row(coupling)
    )
    block = exchange(block.reshape(sets, -1, 1, mols), across).reshape(-1, mols)
    high, low, free, square, amplitudes, momenta, own, place, block = run["first"](place, block, waves)
    amplitudes, momenta, block = run["modes"](exchange(block, inside), amplitudes, momenta, own)
    pull, block = run["middle"](place, exchange(block, inside), free, square, high, low)
    amplitudes, momenta, block = run["modes"](exchange(block, inside), amplitudes, momenta, own)
    positions, velocities, amplitudes, momenta = run["last"](
        place, exchange(block, inside), high, low, pull, free_positions, free_velocities, bond, amplitudes, momenta
    )
    return positions, velocities, amplitudes.T, momenta.T


def solution(mesh):
    bond, mode, mol = P("traj", "mol"), P("mol", "traj"), P("mol")
    return jax.shard_map(
        local,
        mesh=mesh,
        in_specs=(bond, bond, mode, mode, mol, P(), mol, mol, mol, mol, mol),
        out_specs=(bond, bond, mode, mode),
        check_vma=False,
    )
```

```python
import functools

import jax
import jax.numpy as jnp
from jax import lax
from jax.experimental import pallas as pl
from jax.experimental.pallas import tpu as pltpu
from jax.sharding import PartitionSpec as P

STEP_TIME = 0.2
SET = 16
SINE = (25.13273048400879, -64.83467864990234, 67.04389953613281, -38.12319564819336, 12.233302116394043)
F32, BF16 = jnp.float32, jnp.bfloat16
SUB = 8
LANES = 128


def split(x):
    high = x.astype(BF16)
    return high, (x - high.astype(F32)).astype(BF16)


def both(x):
    return jnp.concatenate(split(x), axis=0)


def dot(a, b, axis):
    return lax.dot_general(a, b, (((1,), (axis,)), ((), ())), preferred_element_type=F32)


def product(halves, high, low, axis):
    traj = halves.shape[0] // 2
    first = dot(halves, high, axis)
    return first[:traj] + first[traj:] + dot(halves[:traj], low, axis)


def sine_of(product):
    turn = product.astype(F32) * (2.0**-32)
    square = turn * turn
    value = square * SINE[-1] + SINE[-2]
    for factor in SINE[-3::-1]:
        value = value * square + factor
    return turn * (0.25 - square) * value


def morse(positions, depth, stiffness):
    damped = jnp.exp(-stiffness * positions)
    return -2.0 * depth * stiffness * (1.0 - damped) * damped


def sum_over(ref, part=()):
    total = ref[(0, *part)]
    for i in range(1, ref.shape[0]):
        total = total + ref[(i, *part)]
    return total


def block_rows(traj):
    return 3 * traj + 3 - traj // 2


def start_kernel(positions, velocities, slope, sites, depth, stiffness, amplitudes, momenta, freq, coupling,
                 out_ref, free_positions, free_velocities, bond_ref, *scratch):
    hbm = (positions, velocities, slope, sites, depth, stiffness, amplitudes, momenta, freq, coupling)
    held, sems = scratch[:-1], scratch[-1]
    copies = [pltpu.make_async_copy(a, b, sems.at[i]) for i, (a, b) in enumerate(zip(hbm, held))]
    for copy in copies:
        copy.start()
    for copy in copies:
        copy.wait()
    positions, velocities, slope, sites, depth, stiffness, amplitudes, momenta, freq, coupling = (ref[...] for ref in held)
    traj, owned = amplitudes.shape
    half = traj // 2
    speed = velocities + STEP_TIME * morse(positions, depth, stiffness)
    moved = positions + STEP_TIME * speed
    free_positions[...] = moved
    free_velocities[...] = speed
    bond_ref[...] = jnp.concatenate([slope, depth, stiffness, jnp.zeros((SUB - 3, LANES), F32)], axis=0)
    modes = jnp.concatenate([amplitudes[:half], momenta[:half], amplitudes[half:], momenta[half:]], axis=1)
    own = jnp.concatenate([coupling, freq, coupling, freq], axis=1)
    rows = block_rows(traj)
    for block in range(out_ref.shape[0] // rows):
        at = block * rows
        for piece in (slope * positions, slope * moved, slope, sites.astype(F32), modes, own):
            out_ref[pl.ds(at, piece.shape[0]), :] = piece
            at += piece.shape[0]


def first_kernel(shift, traj, place, column, waves, high_ref, low_ref, free_ref, square_ref, amplitudes_ref, momenta_ref,
                 own_ref, place_out, out_ref, dipole_ref, held_high, held_low):
    place_out[0] = place[0]
    rows = block_rows(traj)
    half = traj // 2
    sets = column.shape[0] // rows
    chunk = out_ref.shape[2]
    owned = chunk // sets
    sites = []
    for q in range(sets):
        at = q * rows
        columns = pl.ds(q * LANES, LANES)
        dipole_ref[:, columns] = both(column[pl.ds(at, traj), :])
        free_ref[:, columns] = column[pl.ds(at + traj, traj), :]
        slope = column[pl.ds(at + 2 * traj, 1), :]
        square_ref[:, columns] = (STEP_TIME * STEP_TIME) * slope * slope
        sites.append(column[pl.ds(at + 2 * traj + 1, 1), :].astype(jnp.int32) << shift)

    def gather(row, count, lane):
        return jnp.concatenate(
            [column[pl.ds(q * rows + row, count), lane * owned : (lane + 1) * owned] for q in range(sets)], axis=1
        )

    at = 2 * traj + 2
    amplitudes_ref[...] = jnp.concatenate([gather(at, half, 0), gather(at, half, 2)], axis=0)
    momenta_ref[...] = jnp.concatenate([gather(at, half, 1), gather(at, half, 3)], axis=0)
    own_ref[...] = jnp.concatenate([gather(at + half, 1, 0), gather(at + half, 1, 1)], axis=0)

    def fill(member, slot):
        taken = pl.ds(pl.multiple_of(member * chunk, chunk), chunk)
        wave = waves[taken, :]
        for q in range(sets):
            high, low = split(sine_of(wave * sites[q]))
            high_ref[q, taken, :] = high
            low_ref[q, taken, :] = low
            held_high[slot, q] = high
            held_low[slot, q] = low

    def finish(member, slot):
        out_ref[member] = product(dipole_ref[...], wide(held_high.at[slot]), wide(held_low.at[slot]), 1)

    def step(pair, carry):
        for slot in range(2):
            finish(2 * pair + slot, slot)
            fill(2 * pair + slot + 1, 1 - slot)
        return carry

    members = out_ref.shape[0]
    fill(0, 0)
    lax.fori_loop(0, members // 2 - 1, step, 0)
    finish(members - 2, 0)
    fill(members - 1, 1)
    finish(members - 1, 1)


def modes_kernel(received, amplitudes, momenta, own, amplitudes_out, momenta_out, out_ref):
    drive = sum_over(received)
    coupling, freq = own[0:1, :], own[1:2, :]
    new_momenta = momenta[...] + STEP_TIME * (-(freq * freq) * amplitudes[...] - coupling * drive)
    new_amplitudes = amplitudes[...] + STEP_TIME * new_momenta
    momenta_out[...] = new_momenta
    amplitudes_out[...] = new_amplitudes
    weighted = coupling * new_amplitudes
    for member in range(out_ref.shape[0]):
        out_ref[member] = weighted


def wide(ref, rows=slice(None)):
    return jnp.concatenate([ref[q, rows, :] for q in range(ref.shape[0])], axis=1)


def pull_of(received, read_high, read_low):
    chunk = received.shape[2]
    pull = None
    for member in range(received.shape[0]):
        rows = pl.ds(member * chunk, chunk)
        piece = product(both(received[member]), read_high(rows), read_low(rows), 0)
        pull = piece if pull is None else pull + piece
    return pull


def middle_kernel(place, received, free_ref, square_ref, high_ref, low_ref, pull_out, out_ref):
    pull = pull_of(received, functools.partial(wide, high_ref), functools.partial(wide, low_ref))
    own = pull[:, :LANES]
    for q in range(1, pull.shape[1] // LANES):
        own = jnp.where(place[0] == q, pull[:, q * LANES : (q + 1) * LANES], own)
    pull_out[...] = own
    dipole = both(free_ref[...] - square_ref[...] * pull)
    chunk = out_ref.shape[2]
    for member in range(out_ref.shape[0]):
        rows = pl.ds(member * chunk, chunk)
        out_ref[member] = product(dipole, wide(high_ref, rows), wide(low_ref, rows), 1)


def last_kernel(place, received, high_ref, low_ref, pull, free_positions, free_velocities, bond_ref, amplitudes, momenta,
                positions_out, velocities_out, amplitudes_out, momenta_out):
    owned = amplitudes_out.shape[1]
    for whole, own in ((amplitudes, amplitudes_out), (momenta, momenta_out)):
        mine = whole[:, :owned]
        for q in range(1, whole.shape[1] // owned):
            mine = jnp.where(place[0] == q, whole[:, q * owned : (q + 1) * owned], mine)
        own[...] = mine
    here = place[0]
    last_pull = pull_of(received, lambda rows: high_ref[here, rows, :], lambda rows: low_ref[here, rows, :])
    slope, depth, stiffness = (bond_ref[i : i + 1, :] for i in range(3))
    first = slope * pull[...]
    velocities = free_velocities[...] - STEP_TIME * first
    positions = free_positions[...] - STEP_TIME * (STEP_TIME * first)
    velocities = velocities + STEP_TIME * (morse(positions, depth, stiffness) - slope * last_pull)
    velocities_out[...] = velocities
    positions_out[...] = positions + STEP_TIME * velocities


def call(kernel, outs, name, spaces, scratch=(), grant=20, interpret=False):
    kinds = {"V": pltpu.VMEM, "S": pltpu.SMEM, "H": pltpu.HBM}
    return pl.pallas_call(
        kernel,
        out_shape=[jax.ShapeDtypeStruct(shape, dtype) for shape, dtype in outs],
        in_specs=[pl.BlockSpec(memory_space=kinds[letter]) for letter in spaces],
        out_specs=[pl.BlockSpec(memory_space=kinds["S" if dtype == jnp.int32 else "V"]) for _, dtype in outs],
        scratch_shapes=list(scratch),
        name=name,
        interpret=interpret,
        compiler_params=None if interpret else pltpu.CompilerParams(vmem_limit_bytes=grant << 20),
    )


def stages(traj, mols, owned, sets, interpret=False):
    lattice = 2 * mols * SET * sets
    shift = 33 - lattice.bit_length()
    modes, chunk, here = sets * SET * owned, sets * owned, sets * mols
    bond, row, own, own_row = (traj, mols), (1, mols), (traj, owned), (1, owned)
    f = lambda *shape: (shape, F32)
    held = [pltpu.VMEM(s, F32) for s in (bond, bond, row)] + [pltpu.VMEM(row, jnp.int32)]
    held += [pltpu.VMEM(s, F32) for s in (row, row, own, own, own_row, own_row)]
    phase = ((sets, modes, mols), BF16)
    state, blocks = f(traj, chunk), f(SET, traj, chunk)
    make = functools.partial(call, interpret=interpret)
    return dict(
        start=make(start_kernel, [f(sets * block_rows(traj), LANES), f(*bond), f(*bond), f(SUB, mols)], "start", 10 * "H",
                   held + [pltpu.SemaphoreType.DMA((len(held),))], grant=56),
        first=make(functools.partial(first_kernel, shift, traj),
                   [phase, phase, f(traj, here), f(1, here), state, state, f(2, chunk), ((1,), jnp.int32), blocks], "first", "SVV",
                   [pltpu.VMEM((2 * traj, here), BF16)] + 2 * [pltpu.VMEM((2, sets, chunk, mols), BF16)]),
        modes=make(modes_kernel, [state, state, blocks], "modes", "VVVV"),
        middle=make(middle_kernel, [f(*bond), blocks], "middle", "SVVVVV"),
        last=make(last_kernel, [f(*bond), f(*bond), f(*own), f(*own)], "last", "S" + 9 * "V"),
    )


def local(positions, velocities, amplitudes, momenta, sites, wavevectors, mode_freq, coupling, depth, stiffness, dipole_slope):
    sets = lax.axis_size("mol") // SET
    traj, mols = positions.shape
    owned = amplitudes.shape[0]
    across = [[q * SET + i for q in range(sets)] for i in range(SET)]
    inside = [[q * SET + i for i in range(SET)] for q in range(sets)]

    def exchange(blocks, groups):
        return lax.all_to_all(blocks, "mol", 0, 0, axis_index_groups=groups, tiled=True)

    run = stages(traj, mols, owned, sets)
    row = lambda x: x.reshape(1, -1)
    place = (lax.axis_index("mol") // SET).astype(jnp.int32).reshape(1)
    waves = wavevectors.reshape(sets, SET, owned).transpose(1, 0, 2).reshape(-1, 1)

    block, free_positions, free_velocities, bond = run["start"](
        positions, velocities, row(dipole_slope), row(sites), row(depth), row(stiffness), amplitudes.T, momenta.T, row(mode_freq), row(coupling)
    )
    block = exchange(block.reshape(sets, -1, 1, mols), across).reshape(-1, mols)
    high, low, free, square, amplitudes, momenta, own, place, block = run["first"](place, block, waves)
    amplitudes, momenta, block = run["modes"](exchange(block, inside), amplitudes, momenta, own)
    pull, block = run["middle"](place, exchange(block, inside), free, square, high, low)
    amplitudes, momenta, block = run["modes"](exchange(block, inside), amplitudes, momenta, own)
    positions, velocities, amplitudes, momenta = run["last"](
        place, exchange(block, inside), high, low, pull, free_positions, free_velocities, bond, amplitudes, momenta
    )
    return positions, velocities, amplitudes.T, momenta.T


def solution(mesh):
    bond, mode, mol = P("traj", "mol"), P("mol", "traj"), P("mol")
    return jax.shard_map(
        local,
        mesh=mesh,
        in_specs=(bond, bond, mode, mode, mol, P(), mol, mol, mol, mol, mol),
        out_specs=(bond, bond, mode, mode),
        check_vma=False,
    )
```

```python
import functools

import jax
import jax.numpy as jnp
from jax import lax
from jax.experimental import pallas as pl
from jax.experimental.pallas import tpu as pltpu
from jax.sharding import PartitionSpec as P

STEP_TIME = 0.2
SET = 16
SINE = (12.695119857788086, -20.77156639099121, 13.623412132263184, -4.913383483886719)
SCALE = 1.2556471824645996
QUARTER = 0.39416247606277466
F32, BF16 = jnp.float32, jnp.bfloat16
SUB = 8
LANES = 128


def split(x):
    high = x.astype(BF16)
    return high, (x - high.astype(F32)).astype(BF16)


def both(x):
    return jnp.concatenate(split(x), axis=0)


def dot(a, b, axis):
    return lax.dot_general(a, b, (((1,), (axis,)), ((), ())), preferred_element_type=F32)


def product(halves, high, low, axis):
    traj = halves.shape[0] // 2
    first = dot(halves, high, axis)
    return first[:traj] + first[traj:] + dot(halves[:traj], low, axis)


def sine_of(product):
    turn = product.astype(F32) * (SCALE * 2.0**-32)
    square = turn * turn
    value = square + SINE[-1]
    for factor in SINE[-2::-1]:
        value = value * square + factor
    return turn * (QUARTER - square) * value


def morse(positions, depth, stiffness):
    damped = jnp.exp(-stiffness * positions)
    return -2.0 * depth * stiffness * (1.0 - damped) * damped


def sum_over(ref, part=()):
    total = ref[(0, *part)]
    for i in range(1, ref.shape[0]):
        total = total + ref[(i, *part)]
    return total


def block_rows(traj):
    return 3 * traj + 3 - traj // 2


def start_kernel(positions, velocities, slope, sites, depth, stiffness, amplitudes, momenta, freq, coupling,
                 out_ref, free_positions, free_velocities, bond_ref, *scratch):
    hbm = (positions, velocities, slope, sites, depth, stiffness, amplitudes, momenta, freq, coupling)
    held, sems = scratch[:-1], scratch[-1]
    copies = [pltpu.make_async_copy(a, b, sems.at[i]) for i, (a, b) in enumerate(zip(hbm, held))]
    for copy in copies:
        copy.start()
    for copy in copies:
        copy.wait()
    positions, velocities, slope, sites, depth, stiffness, amplitudes, momenta, freq, coupling = (ref[...] for ref in held)
    traj, owned = amplitudes.shape
    half = traj // 2
    speed = velocities + STEP_TIME * morse(positions, depth, stiffness)
    moved = positions + STEP_TIME * speed
    free_positions[...] = moved
    free_velocities[...] = speed
    bond_ref[...] = jnp.concatenate([slope, depth, stiffness, jnp.zeros((SUB - 3, LANES), F32)], axis=0)
    modes = jnp.concatenate([amplitudes[:half], momenta[:half], amplitudes[half:], momenta[half:]], axis=1)
    own = jnp.concatenate([coupling, freq, coupling, freq], axis=1)
    rows = block_rows(traj)
    for block in range(out_ref.shape[0] // rows):
        at = block * rows
        for piece in (slope * positions, slope * moved, slope, sites.astype(F32), modes, own):
            out_ref[pl.ds(at, piece.shape[0]), :] = piece
            at += piece.shape[0]


def first_kernel(shift, traj, place, column, waves, high_ref, low_ref, free_ref, square_ref, amplitudes_ref, momenta_ref,
                 own_ref, place_out, out_ref, dipole_ref, held_high, held_low):
    place_out[0] = place[0]
    rows = block_rows(traj)
    half = traj // 2
    sets = column.shape[0] // rows
    chunk = out_ref.shape[2]
    owned = chunk // sets
    sites = []
    for q in range(sets):
        at = q * rows
        columns = pl.ds(q * LANES, LANES)
        dipole_ref[:, columns] = both(column[pl.ds(at, traj), :])
        free_ref[:, columns] = column[pl.ds(at + traj, traj), :]
        slope = column[pl.ds(at + 2 * traj, 1), :]
        square_ref[:, columns] = (STEP_TIME * STEP_TIME) * slope * slope
        sites.append(column[pl.ds(at + 2 * traj + 1, 1), :].astype(jnp.int32) << shift)

    def gather(row, count, lane):
        return jnp.concatenate(
            [column[pl.ds(q * rows + row, count), lane * owned : (lane + 1) * owned] for q in range(sets)], axis=1
        )

    at = 2 * traj + 2
    amplitudes_ref[...] = jnp.concatenate([gather(at, half, 0), gather(at, half, 2)], axis=0)
    momenta_ref[...] = jnp.concatenate([gather(at, half, 1), gather(at, half, 3)], axis=0)
    own_ref[...] = jnp.concatenate([gather(at + half, 1, 0), gather(at + half, 1, 1)], axis=0)

    def fill(member, slot):
        taken = pl.ds(pl.multiple_of(member * chunk, chunk), chunk)
        wave = waves[taken, :]
        for q in range(sets):
            high, low = split(sine_of(wave * sites[q]))
            high_ref[q, taken, :] = high
            low_ref[q, taken, :] = low
            held_high[slot, q] = high
            held_low[slot, q] = low

    def finish(member, slot):
        out_ref[member] = product(dipole_ref[...], wide(held_high.at[slot]), wide(held_low.at[slot]), 1)

    def step(pair, carry):
        for slot in range(2):
            finish(2 * pair + slot, slot)
            fill(2 * pair + slot + 1, 1 - slot)
        return carry

    members = out_ref.shape[0]
    fill(0, 0)
    lax.fori_loop(0, members // 2 - 1, step, 0)
    finish(members - 2, 0)
    fill(members - 1, 1)
    finish(members - 1, 1)


def modes_kernel(received, amplitudes, momenta, own, amplitudes_out, momenta_out, out_ref):
    drive = sum_over(received)
    coupling, freq = own[0:1, :], own[1:2, :]
    new_momenta = momenta[...] + STEP_TIME * (-(freq * freq) * amplitudes[...] - coupling * drive)
    new_amplitudes = amplitudes[...] + STEP_TIME * new_momenta
    momenta_out[...] = new_momenta
    amplitudes_out[...] = new_amplitudes
    weighted = coupling * new_amplitudes
    for member in range(out_ref.shape[0]):
        out_ref[member] = weighted


def wide(ref, rows=slice(None)):
    return jnp.concatenate([ref[q, rows, :] for q in range(ref.shape[0])], axis=1)


def pull_of(received, read_high, read_low):
    chunk = received.shape[2]
    pull = None
    for member in range(received.shape[0]):
        rows = pl.ds(member * chunk, chunk)
        piece = product(both(received[member]), read_high(rows), read_low(rows), 0)
        pull = piece if pull is None else pull + piece
    return pull


def middle_kernel(place, received, free_ref, square_ref, high_ref, low_ref, pull_out, out_ref):
    pull = pull_of(received, functools.partial(wide, high_ref), functools.partial(wide, low_ref))
    own = pull[:, :LANES]
    for q in range(1, pull.shape[1] // LANES):
        own = jnp.where(place[0] == q, pull[:, q * LANES : (q + 1) * LANES], own)
    pull_out[...] = own
    dipole = both(free_ref[...] - square_ref[...] * pull)
    chunk = out_ref.shape[2]
    for member in range(out_ref.shape[0]):
        rows = pl.ds(member * chunk, chunk)
        out_ref[member] = product(dipole, wide(high_ref, rows), wide(low_ref, rows), 1)


def last_kernel(place, received, high_ref, low_ref, pull, free_positions, free_velocities, bond_ref, amplitudes, momenta,
                positions_out, velocities_out, amplitudes_out, momenta_out):
    owned = amplitudes_out.shape[1]
    for whole, own in ((amplitudes, amplitudes_out), (momenta, momenta_out)):
        mine = whole[:, :owned]
        for q in range(1, whole.shape[1] // owned):
            mine = jnp.where(place[0] == q, whole[:, q * owned : (q + 1) * owned], mine)
        own[...] = mine
    here = place[0]
    last_pull = pull_of(received, lambda rows: high_ref[here, rows, :], lambda rows: low_ref[here, rows, :])
    slope, depth, stiffness = (bond_ref[i : i + 1, :] for i in range(3))
    first = slope * pull[...]
    velocities = free_velocities[...] - STEP_TIME * first
    positions = free_positions[...] - STEP_TIME * (STEP_TIME * first)
    velocities = velocities + STEP_TIME * (morse(positions, depth, stiffness) - slope * last_pull)
    velocities_out[...] = velocities
    positions_out[...] = positions + STEP_TIME * velocities


def call(kernel, outs, name, spaces, scratch=(), grant=20, interpret=False):
    kinds = {"V": pltpu.VMEM, "S": pltpu.SMEM, "H": pltpu.HBM}
    return pl.pallas_call(
        kernel,
        out_shape=[jax.ShapeDtypeStruct(shape, dtype) for shape, dtype in outs],
        in_specs=[pl.BlockSpec(memory_space=kinds[letter]) for letter in spaces],
        out_specs=[pl.BlockSpec(memory_space=kinds["S" if dtype == jnp.int32 else "V"]) for _, dtype in outs],
        scratch_shapes=list(scratch),
        name=name,
        interpret=interpret,
        compiler_params=None if interpret else pltpu.CompilerParams(vmem_limit_bytes=grant << 20),
    )


def stages(traj, mols, owned, sets, interpret=False):
    lattice = 2 * mols * SET * sets
    shift = 33 - lattice.bit_length()
    modes, chunk, here = sets * SET * owned, sets * owned, sets * mols
    bond, row, own, own_row = (traj, mols), (1, mols), (traj, owned), (1, owned)
    f = lambda *shape: (shape, F32)
    held = [pltpu.VMEM(s, F32) for s in (bond, bond, row)] + [pltpu.VMEM(row, jnp.int32)]
    held += [pltpu.VMEM(s, F32) for s in (row, row, own, own, own_row, own_row)]
    phase = ((sets, modes, mols), BF16)
    state, blocks = f(traj, chunk), f(SET, traj, chunk)
    make = functools.partial(call, interpret=interpret)
    return dict(
        start=make(start_kernel, [f(sets * block_rows(traj), LANES), f(*bond), f(*bond), f(SUB, mols)], "start", 10 * "H",
                   held + [pltpu.SemaphoreType.DMA((len(held),))], grant=56),
        first=make(functools.partial(first_kernel, shift, traj),
                   [phase, phase, f(traj, here), f(1, here), state, state, f(2, chunk), ((1,), jnp.int32), blocks], "first", "SVV",
                   [pltpu.VMEM((2 * traj, here), BF16)] + 2 * [pltpu.VMEM((2, sets, chunk, mols), BF16)]),
        modes=make(modes_kernel, [state, state, blocks], "modes", "VVVV"),
        middle=make(middle_kernel, [f(*bond), blocks], "middle", "SVVVVV"),
        last=make(last_kernel, [f(*bond), f(*bond), f(*own), f(*own)], "last", "S" + 9 * "V"),
    )


def local(positions, velocities, amplitudes, momenta, sites, wavevectors, mode_freq, coupling, depth, stiffness, dipole_slope):
    sets = lax.axis_size("mol") // SET
    traj, mols = positions.shape
    owned = amplitudes.shape[0]
    across = [[q * SET + i for q in range(sets)] for i in range(SET)]
    inside = [[q * SET + i for i in range(SET)] for q in range(sets)]

    def exchange(blocks, groups):
        return lax.all_to_all(blocks, "mol", 0, 0, axis_index_groups=groups, tiled=True)

    run = stages(traj, mols, owned, sets)
    row = lambda x: x.reshape(1, -1)
    place = (lax.axis_index("mol") // SET).astype(jnp.int32).reshape(1)
    waves = wavevectors.reshape(sets, SET, owned).transpose(1, 0, 2).reshape(-1, 1)

    block, free_positions, free_velocities, bond = run["start"](
        positions, velocities, row(dipole_slope), row(sites), row(depth), row(stiffness), amplitudes.T, momenta.T, row(mode_freq), row(coupling)
    )
    block = exchange(block.reshape(sets, -1, 1, mols), across).reshape(-1, mols)
    high, low, free, square, amplitudes, momenta, own, place, block = run["first"](place, block, waves)
    amplitudes, momenta, block = run["modes"](exchange(block, inside), amplitudes, momenta, own)
    pull, block = run["middle"](place, exchange(block, inside), free, square, high, low)
    amplitudes, momenta, block = run["modes"](exchange(block, inside), amplitudes, momenta, own)
    positions, velocities, amplitudes, momenta = run["last"](
        place, exchange(block, inside), high, low, pull, free_positions, free_velocities, bond, amplitudes, momenta
    )
    return positions, velocities, amplitudes.T, momenta.T


def solution(mesh):
    bond, mode, mol = P("traj", "mol"), P("mol", "traj"), P("mol")
    return jax.shard_map(
        local,
        mesh=mesh,
        in_specs=(bond, bond, mode, mode, mol, P(), mol, mol, mol, mol, mol),
        out_specs=(bond, bond, mode, mode),
        check_vma=False,
    )
```
